32 devices in a mesh: section: 2 (over y), tensor: 4 (over z), ctx: 4 (over x, core).
Axes of the slice: x: 2, y: 2, z: 4, core: 2. Of those that a mesh axis runs over, the one named last changes fastest.
Arguments:
- latents: bfloat16 [3, 1024, 1152], P(None, 'ctx'), may hold values from -6 to 6
- condition: float32 [3, 1152], P(None, 'ctx'), may hold values from -6 to 6
- cotangent: bfloat16 [3, 1024, 1152], P(None, 'ctx'), may hold values from -6 to 6
- w_ada: bfloat16 [2, 1152, 6912], P('section', 'ctx', 'tensor'), may hold values from -0.1875 to 0.1875
- b_ada: float32 [2, 6912], P('section', 'tensor'), may hold values from -3 to 3
- w_qkv: bfloat16 [2, 1152, 3, 1152], P('section', None, None, 'tensor'), may hold values from -0.1875 to 0.1875
- b_qv: float32 [2, 2, 1152], P('section', None, 'tensor'), may hold values from -3 to 3
- w_out: bfloat16 [2, 1152, 1152], P('section', 'tensor'), may hold values from -1.5 to 1.5
- b_out: float32 [2, 1152], P('section'), may hold values from -3 to 3
- w_fc1: bfloat16 [2, 1152, 4608], P('section', None, 'tensor'), may hold values from -0.1875 to 0.1875
- b_fc1: float32 [2, 4608], P('section', 'tensor'), may hold values from -3 to 3
- w_fc2: bfloat16 [2, 4608, 1152], P('section', 'tensor'), may hold values from -0.09375 to 0.09375
- b_fc2: float32 [2, 1152], P('section'), may hold values from -3 to 3
Outputs:
- block_out: bfloat16 [2, 3, 1024, 1152], P('section', None, 'ctx')
- in_grad: float32 [2, 3, 1024, 1152], P('section', None, 'ctx')
- cond_grad: float32 [3, 1152], P(None, 'ctx')
- grad_w_ada: float32 [2, 1152, 6912], P('section', 'ctx', 'tensor')
- grad_b_ada: float32 [2, 6912], P('section', 'tensor')
- grad_w_qkv: float32 [2, 1152, 3, 1152], P('section', 'ctx', None, 'tensor')
- grad_b_qv: float32 [2, 2, 1152], P('section', None, 'tensor')
- grad_w_out: float32 [2, 1152, 1152], P('section', 'tensor', 'ctx')
- grad_b_out: float32 [2, 1152], P('section')
- grad_w_fc1: float32 [2, 1152, 4608], P('section', 'ctx', 'tensor')
- grad_b_fc1: float32 [2, 4608], P('section', 'tensor')
- grad_w_fc2: float32 [2, 4608, 1152], P('section', 'tensor', 'ctx')
- grad_b_fc2: float32 [2, 1152], P('section')
The draws below stay inside these ranges and needn't reach their ends.
All inputs are finite; a program needn't handle non-finite values.
Results may differ from the reference program's by a relative error of at most 0.025.
Values may be sent and summed in bfloat16 or wider, within the bound.
A program may use at most 192 MiB of HBM per device.

```python
import math
import jax
import jax.numpy as jnp
from jax import lax

D = 1152
HEADS = 16
HD = 72
FF = 4608
DC = 1152
SEQ = 1024
LAT = 3
N_TENSOR = 4


def block_levels(stream_key, shape, split, smallest, largest):
    loudness, own = 1.0, jax.random.fold_in(stream_key, 6)
    for axis_at, parts in split:
        steps = jnp.exp(jax.random.uniform(jax.random.fold_in(own, axis_at), (parts,), jnp.float32, smallest / len(split), largest / len(split)))
        loudness = loudness * jnp.repeat(steps, shape[axis_at] // parts).reshape([-1 if axis == axis_at else 1 for axis in range(len(shape))])
    return loudness


def scatter_about(rng, shape, scale, reach, pieces=(), kind=jnp.bfloat16):
    result = scale * jax.random.normal(rng, shape, jnp.float32)
    if pieces:
        result = result * block_levels(rng, shape, pieces, -0.22, 0.18)
    return jnp.clip(result, -reach, reach).astype(kind)


def setup_inputs(seed: int = 0) -> dict:
    splits = jax.random.split(jax.random.key(seed), 14)
    return {
        "latents": scatter_about(splits[0], (LAT, SEQ, D), 1.0, 6.0, ((1, 4),)),
        "condition": scatter_about(splits[1], (LAT, DC), 1.0, 6.0, ((1, 4),), jnp.float32),
        "cotangent": scatter_about(splits[2], (LAT, SEQ, D), 1.0, 6.0, ((1, 4),)),
        "w_ada": scatter_about(splits[3], (2, DC, 6 * D), DC ** -0.5, 0.1875, ((0, 2), (1, 4), (2, 4))),
        "b_ada": scatter_about(splits[4], (2, 6 * D), 0.5, 3.0, ((0, 2), (1, 4)), jnp.float32),
        "w_qkv": scatter_about(splits[5], (2, D, 3, D), D ** -0.5, 0.1875, ((0, 2), (3, 4))),
        "b_qv": scatter_about(splits[6], (2, 2, D), 0.5, 3.0, ((0, 2), (2, 4)), jnp.float32),
        "w_out": scatter_about(splits[7], (2, D, D), (D // 64) ** -0.5, 1.5, ((0, 2), (1, 4))),
        "b_out": scatter_about(splits[8], (2, D), 0.5, 3.0, ((0, 2),), jnp.float32),
        "w_fc1": scatter_about(splits[9], (2, D, FF), D ** -0.5, 0.1875, ((0, 2), (2, 4))),
        "b_fc1": scatter_about(splits[10], (2, FF), 0.5, 3.0, ((0, 2), (1, 4)), jnp.float32),
        "w_fc2": scatter_about(splits[11], (2, FF, D), FF ** -0.5, 0.09375, ((0, 2), (1, 4))),
        "b_fc2": scatter_about(splits[12], (2, D), 0.5, 3.0, ((0, 2),), jnp.float32),
    }


EPSILON = 1e-06

def layer_norm(values):
    centre = lax.optimization_barrier(jnp.mean(values, axis=-1, keepdims=True))
    centred = values - centre
    variance = lax.optimization_barrier(jnp.mean(centred * centred, axis=-1, keepdims=True))
    inverse = lax.rsqrt(variance + EPSILON)
    return (centred * inverse, inverse)

def norm_back(normed, inverse, upstream):
    mean_grad = lax.optimization_barrier(jnp.mean(upstream, axis=-1, keepdims=True))
    mean_cross = lax.optimization_barrier(jnp.mean(upstream * normed, axis=-1, keepdims=True))
    return inverse * (upstream - mean_grad - normed * mean_cross)

def rounded_sum(partials):
    rounded = lax.optimization_barrier(partials.astype(jnp.bfloat16))
    return lax.optimization_barrier(jnp.sum(rounded.astype(jnp.float32), axis=0))

def gelu_back(pre_act, upstream):
    unused_out, pullback = jax.vjp(lambda pre_value: jax.nn.gelu(pre_value, approximate=True), pre_act)
    return pullback(upstream)[0]

def head_view(array):
    return array.astype(jnp.float32).reshape(array.shape[0], HEADS, HD)

def block_forward(inputs, modulation, weights):
    w_qkv, b_qv, w_out, b_out, w_fc1, b_fc1, w_fc2, b_fc2 = weights
    length = inputs.shape[0]
    groups = N_TENSOR
    softmax_scale = 1.0 / math.sqrt(HD)
    residual = inputs.astype(jnp.float32)
    normed_a, inverse_a = layer_norm(residual)
    attn_in = (normed_a * (1.0 + modulation[1]) + modulation[0]).astype(jnp.bfloat16)
    projected = jnp.dot(attn_in, w_qkv.reshape(D, 3 * D), preferred_element_type=jnp.float32).reshape(length, 3, D)
    queries = (projected[:, 0] + b_qv[0]).astype(jnp.bfloat16)
    key_rows = projected[:, 1].astype(jnp.bfloat16)
    values = (projected[:, 2] + b_qv[1]).astype(jnp.bfloat16)
    scores = jnp.einsum('qhd,khd->hqk', head_view(queries), head_view(key_rows)) * softmax_scale
    row_peak = lax.optimization_barrier(jnp.max(scores, axis=-1, keepdims=True))
    log_total = row_peak + jnp.log(lax.optimization_barrier(jnp.sum(jnp.exp(scores - row_peak), axis=-1, keepdims=True)))
    prob_bf = jnp.exp(scores - log_total).astype(jnp.bfloat16)
    context = jnp.einsum('hqk,khd->qhd', prob_bf.astype(jnp.float32), head_view(values)).astype(jnp.bfloat16).reshape(length, D)
    attn_terms = jnp.einsum('sgc,gcd->gsd', context.astype(jnp.float32).reshape(length, groups, D // groups), w_out.astype(jnp.float32).reshape(groups, D // groups, D))
    attn_out = rounded_sum(attn_terms) + b_out
    middle = residual + modulation[2] * attn_out
    normed_m, inverse_m = layer_norm(middle)
    mlp_in = (normed_m * (1.0 + modulation[4]) + modulation[3]).astype(jnp.bfloat16)
    pre_act = jnp.dot(mlp_in, w_fc1, preferred_element_type=jnp.float32) + b_fc1
    hidden = jax.nn.gelu(pre_act, approximate=True).astype(jnp.bfloat16)
    mlp_terms = jnp.einsum('sgf,gfd->gsd', hidden.astype(jnp.float32).reshape(length, groups, FF // groups), w_fc2.astype(jnp.float32).reshape(groups, FF // groups, D))
    mlp_out = rounded_sum(mlp_terms) + b_fc2
    output = (middle + modulation[5] * mlp_out).astype(jnp.bfloat16)
    stored = (normed_a, inverse_a, attn_in, queries, key_rows, values, log_total, context, attn_out, normed_m, inverse_m, mlp_in, pre_act, hidden, mlp_out)
    return (output, stored)

def block_backward(upstream, stored, modulation, weights):
    w_qkv, b_qv, w_out, b_out, w_fc1, b_fc1, w_fc2, b_fc2 = weights
    normed_a, inverse_a, attn_in, queries, key_rows, values, log_total, context, attn_out, normed_m, inverse_m, mlp_in, pre_act, hidden, mlp_out = stored
    length = upstream.shape[0]
    groups = N_TENSOR
    softmax_scale = 1.0 / math.sqrt(HD)
    gate_m_grad = lax.optimization_barrier(jnp.sum(upstream * mlp_out, axis=0))
    mlp_grad = upstream * modulation[5]
    mlp_grad_b = mlp_grad.astype(jnp.bfloat16)
    grad_w2 = jnp.dot(hidden.T, mlp_grad_b, preferred_element_type=jnp.float32)
    grad_b2 = lax.optimization_barrier(jnp.sum(mlp_grad, axis=0))
    pre_grad = gelu_back(pre_act, jnp.dot(mlp_grad_b, w_fc2.T, preferred_element_type=jnp.float32))
    pre_grad_b = pre_grad.astype(jnp.bfloat16)
    grad_w1 = jnp.dot(mlp_in.T, pre_grad_b, preferred_element_type=jnp.float32)
    grad_b1 = lax.optimization_barrier(jnp.sum(pre_grad, axis=0))
    mlp_in_grad = rounded_sum(jnp.einsum('sgf,dgf->gsd', pre_grad_b.astype(jnp.float32).reshape(length, groups, FF // groups), w_fc1.astype(jnp.float32).reshape(D, groups, FF // groups)))
    shift_m_grad = lax.optimization_barrier(jnp.sum(mlp_in_grad, axis=0))
    scale_m_grad = lax.optimization_barrier(jnp.sum(mlp_in_grad * normed_m, axis=0))
    middle_grad = upstream + norm_back(normed_m, inverse_m, mlp_in_grad * (1.0 + modulation[4]))
    gate_a_grad = lax.optimization_barrier(jnp.sum(middle_grad * attn_out, axis=0))
    attn_grad = middle_grad * modulation[2]
    attn_grad_b = attn_grad.astype(jnp.bfloat16)
    grad_wo = jnp.dot(context.T, attn_grad_b, preferred_element_type=jnp.float32)
    grad_bo = lax.optimization_barrier(jnp.sum(attn_grad, axis=0))
    context_grad = jnp.dot(attn_grad_b, w_out.T, preferred_element_type=jnp.float32).astype(jnp.bfloat16)
    query_heads = head_view(queries)
    key_heads = head_view(key_rows)
    scores = jnp.einsum('qhd,khd->hqk', query_heads, key_heads) * softmax_scale
    prob_full = jnp.exp(scores - log_total)
    prob_bf = prob_full.astype(jnp.bfloat16)
    grad_heads = head_view(context_grad)
    prob_grad = jnp.einsum('qhd,khd->hqk', grad_heads, head_view(values))
    delta_rows = lax.optimization_barrier(jnp.sum(grad_heads * head_view(context), axis=-1)).T[:, :, None]
    score_grad = (prob_full * (prob_grad - delta_rows)).astype(jnp.bfloat16).astype(jnp.float32)
    query_grad = (jnp.einsum('hqk,khd->qhd', score_grad, key_heads) * softmax_scale).reshape(length, D)
    key_grad = (jnp.einsum('hqk,qhd->khd', score_grad, query_heads) * softmax_scale).reshape(length, D)
    value_grad = jnp.einsum('hqk,qhd->khd', prob_bf.astype(jnp.float32), grad_heads).reshape(length, D)
    grad_bqv = jnp.stack([lax.optimization_barrier(jnp.sum(query_grad, axis=0)), lax.optimization_barrier(jnp.sum(value_grad, axis=0))])
    qkv_grad_b = jnp.stack([query_grad, key_grad, value_grad], axis=1).astype(jnp.bfloat16)
    grad_wqkv = jnp.dot(attn_in.T, qkv_grad_b.reshape(length, 3 * D), preferred_element_type=jnp.float32).reshape(D, 3, D)
    attn_in_grad = rounded_sum(jnp.einsum('sjgc,djgc->gsd', qkv_grad_b.astype(jnp.float32).reshape(length, 3, groups, D // groups), w_qkv.astype(jnp.float32).reshape(D, 3, groups, D // groups)))
    shift_a_grad = lax.optimization_barrier(jnp.sum(attn_in_grad, axis=0))
    scale_a_grad = lax.optimization_barrier(jnp.sum(attn_in_grad * normed_a, axis=0))
    input_grad = middle_grad + norm_back(normed_a, inverse_a, attn_in_grad * (1.0 + modulation[1]))
    mod_grad = jnp.stack([shift_a_grad, scale_a_grad, gate_a_grad, shift_m_grad, scale_m_grad, gate_m_grad])
    return (input_grad, mod_grad, (grad_wqkv, grad_bqv, grad_wo, grad_bo, grad_w1, grad_b1, grad_w2, grad_b2))

def reference(latents, condition, cotangent, w_ada, b_ada, w_qkv, b_qv, w_out, b_out, w_fc1, b_fc1, w_fc2, b_fc2):
    cond_act = jax.nn.silu(condition).astype(jnp.bfloat16)
    section_weights = [tuple((weight[block_id] for weight in (w_qkv, b_qv, w_out, b_out, w_fc1, b_fc1, w_fc2, b_fc2))) for block_id in range(2)]
    modulation = [(jnp.dot(cond_act, w_ada[block_id], preferred_element_type=jnp.float32) + b_ada[block_id]).reshape(LAT, 6, D) for block_id in range(2)]

    def run_forward(block_id, inputs):
        params = section_weights[block_id]
        return lax.map(lambda pair: block_forward(pair[0], pair[1], params)[0], (inputs, modulation[block_id]))

    def run_backward(block_id, inputs, upstream):
        params = section_weights[block_id]

        def step_fn(carry, item):
            block_in, mod_latent, grad_latent = item
            unused_out, stored = block_forward(block_in, mod_latent, params)
            input_grad, mod_grad, grad_terms = block_backward(grad_latent, stored, mod_latent, params)
            return (jax.tree.map(jnp.add, carry, grad_terms), (input_grad, mod_grad))
        zeros_init = tuple((jnp.zeros(weight.shape, jnp.float32) for weight in params))
        return lax.scan(step_fn, zeros_init, (inputs, modulation[block_id], upstream))
    first_out = run_forward(0, latents)
    second_out = run_forward(1, first_out)
    second_grads, (second_in_grad, second_mod) = run_backward(1, first_out, cotangent.astype(jnp.float32))
    first_grads, (first_in_grad, first_mod) = run_backward(0, latents, second_in_grad)
    mod_grads = [first_mod.reshape(LAT, 6 * D), second_mod.reshape(LAT, 6 * D)]
    mod_rounded = [grad_mod.astype(jnp.bfloat16) for grad_mod in mod_grads]
    grad_w_ada = jnp.stack([jnp.dot(cond_act.T, mod_rounded[block_id], preferred_element_type=jnp.float32) for block_id in range(2)])
    grad_b_ada = jnp.stack([lax.optimization_barrier(jnp.sum(mod_grads[block_id], axis=0)) for block_id in range(2)])
    cond_sum = jnp.dot(mod_rounded[0], w_ada[0].T, preferred_element_type=jnp.float32) + jnp.dot(mod_rounded[1], w_ada[1].T, preferred_element_type=jnp.float32)
    sigmoid_c = jax.nn.sigmoid(condition)
    cond_grad = cond_sum * sigmoid_c * (1.0 + condition * (1.0 - sigmoid_c))
    stacked = [jnp.stack([first_grads[which], second_grads[which]]) for which in range(8)]
    return (jnp.stack([first_out, second_out]), jnp.stack([first_in_grad, second_in_grad]), cond_grad, grad_w_ada, grad_b_ada, stacked[0], stacked[1], stacked[2], stacked[3], stacked[4], stacked[5], stacked[6], stacked[7])
```

```python
import functools
import math

import jax
import jax.numpy as jnp
from jax import lax
from jax.experimental import pallas as pl
from jax.experimental.pallas import tpu as pltpu
from jax.sharding import PartitionSpec as P

HD = 72
MB = 1
NMB = 3


EPSILON = 1e-06


MESH = pl.DeviceIdType.MESH
PIECES = 2


def line_role(d, n, pieces, rows, x_ref, out_ref, acc, buf_l, buf_r, sems):
    send_r, send_l, recv_l, recv_r, back_send_r, back_send_l, back_recv = sems

    def part(j, s):
        return pl.ds((j * pieces + s) * rows, rows)

    def hop(src, dst, send_sem, recv_sem, to):
        return pltpu.make_async_remote_copy(
            src_ref=src,
            dst_ref=dst,
            send_sem=send_sem,
            recv_sem=recv_sem,
            device_id={"tensor": to},
            device_id_type=MESH,
        )

    def to_right(j, s, src):
        span = part(j, s)
        return hop(
            src.at[span], buf_l.at[span], send_r.at[j, s], recv_l.at[j, s], min(d + 1, n - 1)
        )

    def to_left(j, s, src):
        span = part(j, s)
        return hop(src.at[span], buf_r.at[span], send_l.at[j, s], recv_r.at[j, s], max(d - 1, 0))

    def back_right(j, s):
        span = part(j, s)
        return hop(
            out_ref.at[span],
            out_ref.at[span],
            back_send_r.at[j, s],
            back_recv.at[j, s],
            min(d + 1, n - 1),
        )

    def back_left(j, s):
        span = part(j, s)
        return hop(
            out_ref.at[span],
            out_ref.at[span],
            back_send_l.at[j, s],
            back_recv.at[j, s],
            max(d - 1, 0),
        )

    def done_at(j, s):
        return max(
            2 * j + (n - 1 - j) * pieces + s,
            2 * (n - 1 - j) + j * pieces + s,
        )

    steps = []
    for s in range(pieces):
        for j in range(d + 1, n):
            steps.append((2 * d + (n - 1 - j) * pieces + s, 0, j, s))
            steps.append((done_at(j, s) + 2 * (j - d), 3, j, s))
        for j in range(d):
            steps.append((2 * (n - 1 - d) + j * pieces + s, 1, j, s))
            steps.append((done_at(j, s) + 2 * (d - j), 3, j, s))
        steps.append((done_at(d, s), 2, d, s))
    steps.sort()
    sent = []
    for when, kind, j, s in steps:
        span = part(j, s)
        if kind == 0:
            src = x_ref
            if d > 0:
                to_right(j, s, x_ref).wait_recv()
                acc[span] = (
                    x_ref[span].astype(jnp.float32) + buf_l[span].astype(jnp.float32)
                ).astype(acc.dtype)
                src = acc
            sent.append(to_right(j, s, src))
            sent[-1].start()
        elif kind == 1:
            src = x_ref
            if d < n - 1:
                to_left(j, s, x_ref).wait_recv()
                acc[span] = (
                    x_ref[span].astype(jnp.float32) + buf_r[span].astype(jnp.float32)
                ).astype(acc.dtype)
                src = acc
            sent.append(to_left(j, s, src))
            sent[-1].start()
        elif kind == 2:
            total = x_ref[span].astype(jnp.float32)
            if d > 0:
                to_right(j, s, x_ref).wait_recv()
                total = total + buf_l[span].astype(jnp.float32)
            if d < n - 1:
                to_left(j, s, x_ref).wait_recv()
                total = total + buf_r[span].astype(jnp.float32)
            out_ref[span] = total.astype(out_ref.dtype)
            if d < n - 1:
                sent.append(back_right(j, s))
                sent[-1].start()
            if d > 0:
                sent.append(back_left(j, s))
                sent[-1].start()
        else:
            back_right(j, s).wait_recv()
            if j < d and d < n - 1:
                sent.append(back_right(j, s))
                sent[-1].start()
            if j > d and d > 0:
                sent.append(back_left(j, s))
                sent[-1].start()
    for copy in sent:
        copy.wait_send()


def line_sum_kernel(n, pieces, rows, x_ref, out_ref, acc, buf_l, buf_r, *sems):
    me = lax.axis_index("tensor")
    barrier = pltpu.get_barrier_semaphore()
    for d in range(n):

        @pl.when(me == d)
        def role():
            near = [at for at in (d - 1, d + 1) if 0 <= at < n]
            for at in near:
                pl.semaphore_signal(
                    barrier, inc=1, device_id={"tensor": at}, device_id_type=MESH
                )
            pl.semaphore_wait(barrier, len(near))
            line_role(d, n, pieces, rows, x_ref, out_ref, acc, buf_l, buf_r, sems)


def tensor_sum(term):
    n = lax.axis_size("tensor")
    if n == 1:
        return term
    total_rows, columns = term.shape
    rows = total_rows // (n * PIECES)
    sem = pltpu.SemaphoreType.DMA((n, PIECES))
    return pl.pallas_call(
        functools.partial(line_sum_kernel, n, PIECES, rows),
        out_shape=jax.ShapeDtypeStruct(term.shape, term.dtype),
        in_specs=[pl.BlockSpec(memory_space=pltpu.VMEM)],
        out_specs=pl.BlockSpec(memory_space=pltpu.VMEM),
        scratch_shapes=[pltpu.VMEM(term.shape, term.dtype)] * 3 + [sem] * 7,
        compiler_params=pltpu.CompilerParams(collective_id=0, has_side_effects=True),
        name="tensor_sum",
    )(term)


def owner_sum_kernel(n, rows, x_ref, out_ref, held, send_sem, recv_sem):
    me = lax.axis_index("ctx")
    barrier = pltpu.get_barrier_semaphore()
    for step in range(1, n):
        pl.semaphore_signal(
            barrier, inc=1, device_id={"ctx": lax.rem(me + step, n)}, device_id_type=MESH
        )
    pl.semaphore_wait(barrier, n - 1)
    copies = []
    for step in range(1, n):
        peer = lax.rem(me + step, n)
        copy = pltpu.make_async_remote_copy(
            src_ref=x_ref.at[pl.ds(pl.multiple_of(peer * rows, rows), rows)],
            dst_ref=held.at[step - 1],
            send_sem=send_sem.at[step - 1],
            recv_sem=recv_sem.at[step - 1],
            device_id={"ctx": peer},
            device_id_type=MESH,
        )
        copy.start()
        copies.append(copy)
    own = pl.ds(pl.multiple_of(me * rows, rows), rows)
    out_ref[...] = x_ref[own].astype(jnp.float32)
    for step in range(1, n):
        copies[step - 1].wait_recv()
        out_ref[...] += held[step - 1].astype(jnp.float32)
    for copy in copies:
        copy.wait_send()


def owner_sum(parts):
    n = lax.axis_size("ctx")
    if n == 1:
        return parts.astype(jnp.float32)
    total_rows, columns = parts.shape
    rows = total_rows // n
    sem = pltpu.SemaphoreType.DMA((n - 1,))
    return pl.pallas_call(
        functools.partial(owner_sum_kernel, n, rows),
        out_shape=jax.ShapeDtypeStruct((rows, columns), jnp.float32),
        in_specs=[pl.BlockSpec(memory_space=pltpu.VMEM)],
        out_specs=pl.BlockSpec(memory_space=pltpu.VMEM),
        scratch_shapes=[pltpu.VMEM((n - 1, rows, columns), parts.dtype), sem, sem],
        compiler_params=pltpu.CompilerParams(collective_id=1, has_side_effects=True),
        name="owner_sum",
    )(parts)


def passed_along(shard, axis, by):
    devices = lax.axis_size(axis)
    pairs = [(i, i + by) for i in range(devices) if 0 <= i + by < devices]
    return lax.ppermute(shard, axis, pairs)


def layer_norm(values):
    centre = jnp.mean(values, axis=-1, keepdims=True)
    centred = values - centre
    variance = jnp.mean(centred * centred, axis=-1, keepdims=True)
    inverse = lax.rsqrt(variance + EPSILON)
    return (centred * inverse, inverse)


def norm_back(normed, inverse, upstream):
    mean_grad = jnp.mean(upstream, axis=-1, keepdims=True)
    mean_cross = jnp.mean(upstream * normed, axis=-1, keepdims=True)
    return inverse * (upstream - mean_grad - normed * mean_cross)


def gelu_back(pre_act, upstream):
    unused_out, pullback = jax.vjp(
        lambda pre_value: jax.nn.gelu(pre_value, approximate=True), pre_act
    )
    return pullback(upstream)[0]


def head_view(array):
    return array.reshape(array.shape[0], array.shape[1], array.shape[2] // HD, HD)


def attend(queries, keys_all, values_all):
    softmax_scale = 1.0 / math.sqrt(HD)
    scores = (
        jnp.einsum(
            "bqhd,bkhd->bhqk",
            head_view(queries),
            head_view(keys_all),
            preferred_element_type=jnp.float32,
        )
        * softmax_scale
    )
    row_peak = jnp.max(scores, axis=-1, keepdims=True)
    log_total = row_peak + jnp.log(jnp.sum(jnp.exp(scores - row_peak), axis=-1, keepdims=True))
    prob_bf = jnp.exp(scores - log_total).astype(jnp.bfloat16)
    context = jnp.einsum(
        "bhqk,bkhd->bqhd", prob_bf, head_view(values_all), preferred_element_type=jnp.float32
    )
    return (context.astype(jnp.bfloat16).reshape(queries.shape), log_total)


def row_delta(context, context_grad):
    delta_rows = jnp.sum(
        head_view(context_grad).astype(jnp.float32) * head_view(context).astype(jnp.float32),
        axis=-1,
    )
    return jnp.transpose(delta_rows, (0, 2, 1))[..., None]


def score_terms(query_heads, key_heads, value_heads, grad_heads, log_total, delta_rows):
    softmax_scale = 1.0 / math.sqrt(HD)
    scores = (
        jnp.einsum("bqhd,bkhd->bhqk", query_heads, key_heads, preferred_element_type=jnp.float32)
        * softmax_scale
    )
    prob_full = jnp.exp(scores - log_total)
    prob_grad = jnp.einsum(
        "bqhd,bkhd->bhqk", grad_heads, value_heads, preferred_element_type=jnp.float32
    )
    score_grad = (prob_full * (prob_grad - delta_rows)).astype(jnp.bfloat16)
    return (prob_full, score_grad)


def key_side(query_heads, grad_heads, prob_full, score_grad, key_shape):
    softmax_scale = 1.0 / math.sqrt(HD)
    prob_bf = prob_full.astype(jnp.bfloat16)
    key_part = (
        jnp.einsum("bhqk,bqhd->bkhd", score_grad, query_heads, preferred_element_type=jnp.float32)
        * softmax_scale
    )
    value_part = jnp.einsum(
        "bhqk,bqhd->bkhd", prob_bf, grad_heads, preferred_element_type=jnp.float32
    )
    return (key_part.reshape(key_shape), value_part.reshape(key_shape))


def attention_grads(queries, keys_all, values_all, log_total, context, context_grad):
    softmax_scale = 1.0 / math.sqrt(HD)
    query_heads = head_view(queries)
    key_heads = head_view(keys_all)
    grad_heads = head_view(context_grad)
    delta_rows = row_delta(context, context_grad)
    prob_full, score_grad = score_terms(
        query_heads, key_heads, head_view(values_all), grad_heads, log_total, delta_rows
    )
    query_grad = (
        jnp.einsum("bhqk,bkhd->bqhd", score_grad, key_heads, preferred_element_type=jnp.float32)
        * softmax_scale
    ).reshape(queries.shape)
    key_part, value_part = key_side(query_heads, grad_heads, prob_full, score_grad, keys_all.shape)
    cols = queries.shape[-1]
    both = jnp.concatenate([key_part, value_part], axis=-1).astype(jnp.bfloat16)
    owned = owner_sum(both.reshape(-1, 2 * cols)).reshape(*queries.shape[:2], 2 * cols)
    key_grad, value_grad = owned[..., :cols], owned[..., cols:]
    return (query_grad, key_grad, value_grad)


def forward_block(block_in, mod_rows, weights):
    w_qkv, b_qv, w_out, b_out, w_fc1, b_fc1, w_fc2, b_fc2 = weights
    latent_count, token_count, model_width = block_in.shape
    row_count = latent_count * token_count
    local_cols = w_qkv.shape[-1]
    residual = block_in.astype(jnp.float32)
    normed_a, inverse_a = layer_norm(residual)
    attn_in = (normed_a * (1.0 + mod_rows[:, 1, None, :]) + mod_rows[:, 0, None, :]).astype(
        jnp.bfloat16
    )
    projected = jnp.dot(
        attn_in.reshape(row_count, model_width),
        w_qkv.reshape(model_width, 3 * local_cols),
        preferred_element_type=jnp.float32,
    ).reshape(latent_count, token_count, 3, local_cols)
    queries = (projected[:, :, 0] + b_qv[0]).astype(jnp.bfloat16)
    key_rows = projected[:, :, 1].astype(jnp.bfloat16)
    values = (projected[:, :, 2] + b_qv[1]).astype(jnp.bfloat16)
    both = lax.all_gather(
        jnp.concatenate([key_rows, values], axis=-1), "ctx", axis=1, tiled=True
    )
    keys_all, values_all = both[..., :local_cols], both[..., local_cols:]
    context, log_total = attend(queries, keys_all, values_all)
    attn_term = jnp.dot(
        context.reshape(row_count, local_cols), w_out, preferred_element_type=jnp.float32
    )
    attn_out = (
        tensor_sum(attn_term.astype(jnp.bfloat16))
        .astype(jnp.float32)
        .reshape(block_in.shape)
        + b_out
    )
    middle = residual + mod_rows[:, 2, None, :] * attn_out
    normed_m, inverse_m = layer_norm(middle)
    mlp_in = (normed_m * (1.0 + mod_rows[:, 4, None, :]) + mod_rows[:, 3, None, :]).astype(
        jnp.bfloat16
    )
    pre_act = (
        jnp.dot(mlp_in.reshape(row_count, model_width), w_fc1, preferred_element_type=jnp.float32)
        + b_fc1
    )
    hidden = jax.nn.gelu(pre_act, approximate=True).astype(jnp.bfloat16)
    mlp_term = jnp.dot(hidden, w_fc2, preferred_element_type=jnp.float32)
    mlp_out = (
        tensor_sum(mlp_term.astype(jnp.bfloat16))
        .astype(jnp.float32)
        .reshape(block_in.shape)
        + b_fc2
    )
    block_res = (middle + mod_rows[:, 5, None, :] * mlp_out).astype(jnp.bfloat16)
    stored = (
        normed_a,
        inverse_a,
        attn_in,
        queries,
        keys_all,
        values_all,
        log_total,
        context,
        attn_out,
        normed_m,
        inverse_m,
        mlp_in,
        pre_act,
        hidden,
        mlp_out,
    )
    return (block_res, stored)


def backward_block(upstream, stored, mod_rows, weights):
    w_qkv, b_qv, w_out, b_out, w_fc1, b_fc1, w_fc2, b_fc2 = weights
    (
        normed_a,
        inverse_a,
        attn_in,
        queries,
        keys_all,
        values_all,
        log_total,
        context,
        attn_out,
        normed_m,
        inverse_m,
        mlp_in,
        pre_act,
        hidden,
        mlp_out,
    ) = stored
    latent_count, token_count, model_width = upstream.shape
    row_count = latent_count * token_count
    local_cols = queries.shape[-1]
    gate_m_grad = jnp.sum(upstream * mlp_out, axis=1)
    mlp_grad = upstream * mod_rows[:, 5, None, :]
    mlp_grad_b = mlp_grad.reshape(row_count, model_width).astype(jnp.bfloat16)
    grad_b2 = jnp.sum(mlp_grad, axis=(0, 1))
    pre_grad = gelu_back(pre_act, jnp.dot(mlp_grad_b, w_fc2.T, preferred_element_type=jnp.float32))
    pre_grad_b = pre_grad.astype(jnp.bfloat16)
    grad_b1 = jnp.sum(pre_grad, axis=0)
    mlp_in_grad = (
        tensor_sum(
            jnp.dot(pre_grad_b, w_fc1.T, preferred_element_type=jnp.float32).astype(jnp.bfloat16)
        )
        .astype(jnp.float32)
        .reshape(upstream.shape)
    )
    shift_m_grad = jnp.sum(mlp_in_grad, axis=1)
    scale_m_grad = jnp.sum(mlp_in_grad * normed_m, axis=1)
    middle_grad = upstream + norm_back(
        normed_m, inverse_m, mlp_in_grad * (1.0 + mod_rows[:, 4, None, :])
    )
    gate_a_grad = jnp.sum(middle_grad * attn_out, axis=1)
    attn_grad = middle_grad * mod_rows[:, 2, None, :]
    attn_grad_b = attn_grad.reshape(row_count, model_width).astype(jnp.bfloat16)
    grad_bo = jnp.sum(attn_grad, axis=(0, 1))
    context_grad = (
        jnp.dot(attn_grad_b, w_out.T, preferred_element_type=jnp.float32)
        .astype(jnp.bfloat16)
        .reshape(queries.shape)
    )
    query_grad, key_grad, value_grad = attention_grads(
        queries, keys_all, values_all, log_total, context, context_grad
    )
    grad_bqv = jnp.stack([jnp.sum(query_grad, axis=(0, 1)), jnp.sum(value_grad, axis=(0, 1))])
    qkv_grad_b = (
        jnp.stack([query_grad, key_grad, value_grad], axis=2)
        .astype(jnp.bfloat16)
        .reshape(row_count, 3 * local_cols)
    )
    attn_in_grad = (
        tensor_sum(
            jnp.dot(
                qkv_grad_b,
                w_qkv.reshape(model_width, 3 * local_cols).T,
                preferred_element_type=jnp.float32,
            ).astype(jnp.bfloat16)
        )
        .astype(jnp.float32)
        .reshape(upstream.shape)
    )
    shift_a_grad = jnp.sum(attn_in_grad, axis=1)
    scale_a_grad = jnp.sum(attn_in_grad * normed_a, axis=1)
    input_grad = middle_grad + norm_back(
        normed_a, inverse_a, attn_in_grad * (1.0 + mod_rows[:, 1, None, :])
    )
    mod_grad = jnp.stack(
        [shift_a_grad, scale_a_grad, gate_a_grad, shift_m_grad, scale_m_grad, gate_m_grad], axis=1
    )
    return (
        input_grad,
        mod_grad,
        (grad_bqv, grad_bo, grad_b1, grad_b2),
        (
            (attn_in.reshape(row_count, model_width), qkv_grad_b),
            (context.reshape(row_count, local_cols), attn_grad_b),
            (mlp_in.reshape(row_count, model_width), pre_grad_b),
            (hidden, mlp_grad_b),
        ),
    )


def local(
    latents,
    condition,
    cotangent,
    w_ada,
    b_ada,
    w_qkv,
    b_qv,
    w_out,
    b_out,
    w_fc1,
    b_fc1,
    w_fc2,
    b_fc2,
):
    weights = (w_qkv[0], b_qv[0], w_out[0], b_out[0], w_fc1[0], b_fc1[0], w_fc2[0], b_fc2[0])
    section_index = lax.axis_index("section")
    latent_total, token_count, model_width = latents.shape
    width_cols = b_ada.shape[-1]
    col_offset = lax.axis_index("tensor") * width_cols
    cond_act = jax.nn.silu(condition).astype(jnp.bfloat16)
    mod_part = jnp.dot(cond_act, w_ada[0], preferred_element_type=jnp.float32)
    mod_local = lax.psum(mod_part, "ctx") + b_ada[0]
    modulation = lax.all_gather(mod_local, "tensor", axis=1, tiled=True).reshape(
        latent_total, 6, model_width
    )
    received = jnp.zeros((MB, token_count, model_width), jnp.bfloat16)
    block_out = jnp.zeros_like(latents)
    kept_states = []
    for forward_tick in range(NMB + 1):
        micro_index = forward_tick - section_index
        is_valid = (micro_index >= 0) & (micro_index < NMB)
        offset = jnp.clip(micro_index, 0, NMB - 1) * MB
        own_rows = lax.dynamic_slice_in_dim(latents, offset, MB, 0)
        block_in = jnp.where(section_index == 0, own_rows, received)
        mod_rows = lax.dynamic_slice_in_dim(modulation, offset, MB, 0)
        block_res, stored = forward_block(block_in, mod_rows, weights)
        kept_states.append(stored)
        previous = lax.dynamic_slice_in_dim(block_out, offset, MB, 0)
        block_out = lax.dynamic_update_slice_in_dim(
            block_out, jnp.where(is_valid, block_res, previous), offset, 0
        )
        if forward_tick < NMB:
            received = passed_along(block_res, "section", 1)
    in_grads = jnp.zeros(latents.shape, jnp.float32)
    mod_grads = jnp.zeros((latent_total, width_cols), jnp.float32)
    pairs = []
    small_local = tuple(
        (
            jnp.zeros(weight.shape, jnp.float32)
            for weight in (weights[1], weights[3], weights[5], weights[7])
        )
    )
    grad_received = jnp.zeros((MB, token_count, model_width), jnp.float32)
    for back_tick in range(NMB + 1):
        forward_tick = NMB - back_tick
        micro_index = forward_tick - section_index
        is_valid = (micro_index >= 0) & (micro_index < NMB)
        offset = jnp.clip(micro_index, 0, NMB - 1) * MB
        own_cot = lax.dynamic_slice_in_dim(cotangent, offset, MB, 0).astype(jnp.float32)
        upstream = jnp.where(section_index == 1, own_cot, grad_received)
        mod_rows = lax.dynamic_slice_in_dim(modulation, offset, MB, 0)
        stored = kept_states[forward_tick]
        input_grad, mod_grad, grad_terms, grad_pairs = backward_block(
            upstream, stored, mod_rows, weights
        )
        pairs.append(
            tuple(
                (left, jnp.where(is_valid, right, jnp.zeros_like(right)))
                for left, right in grad_pairs
            )
        )
        masked = tuple((jnp.where(is_valid, term, 0.0) for term in grad_terms))
        previous = lax.dynamic_slice_in_dim(in_grads, offset, MB, 0)
        in_grads = lax.dynamic_update_slice_in_dim(
            in_grads, jnp.where(is_valid, input_grad, previous), offset, 0
        )
        mod_piece = lax.dynamic_slice_in_dim(
            mod_grad.reshape(MB, 6 * model_width), col_offset, width_cols, 1
        )
        prior = lax.dynamic_slice_in_dim(mod_grads, offset, MB, 0)
        mod_grads = lax.dynamic_update_slice_in_dim(
            mod_grads, jnp.where(is_valid, mod_piece, prior), offset, 0
        )
        small_local = tuple(total + term for total, term in zip(small_local, masked))
        if back_tick < NMB:
            grad_received = passed_along(input_grad.astype(jnp.bfloat16), "section", -1).astype(
                input_grad.dtype
            )
    big_local = tuple(
        jnp.dot(
            jnp.concatenate([tick[which][0] for tick in pairs], axis=0).T,
            jnp.concatenate([tick[which][1] for tick in pairs], axis=0),
            preferred_element_type=jnp.float32,
        )
        for which in range(4)
    )
    big_local = (big_local[0].reshape(weights[0].shape),) + big_local[1:]
    shares = (
        lax.psum_scatter(
            big_local[0].astype(jnp.bfloat16), "ctx", scatter_dimension=0, tiled=True
        ).astype(jnp.float32),
        lax.psum_scatter(
            big_local[1].astype(jnp.bfloat16), "ctx", scatter_dimension=1, tiled=True
        ).astype(jnp.float32),
        lax.psum_scatter(
            big_local[2].astype(jnp.bfloat16), "ctx", scatter_dimension=0, tiled=True
        ).astype(jnp.float32),
        lax.psum_scatter(
            big_local[3].astype(jnp.bfloat16), "ctx", scatter_dimension=1, tiled=True
        ).astype(jnp.float32),
    )
    small_sums = lax.psum(
        (mod_grads, small_local[0], small_local[1], small_local[2], small_local[3]), "ctx"
    )
    mod_total = small_sums[0]
    mod_rounded = mod_total.astype(jnp.bfloat16)
    grad_w_ada = jnp.dot(cond_act.T, mod_rounded, preferred_element_type=jnp.float32)[None]
    grad_b_ada = jnp.sum(mod_total, axis=0)[None]
    cond_part = jnp.dot(mod_rounded, w_ada[0].T, preferred_element_type=jnp.float32)
    cond_sum = lax.psum(cond_part, ("section", "tensor"))
    sigmoid_c = jax.nn.sigmoid(condition)
    cond_grad = cond_sum * sigmoid_c * (1.0 + condition * (1.0 - sigmoid_c))
    return (
        block_out[None],
        in_grads[None],
        cond_grad,
        grad_w_ada,
        grad_b_ada,
        shares[0][None],
        small_sums[1][None],
        shares[1][None],
        small_sums[2][None],
        shares[2][None],
        small_sums[3][None],
        shares[3][None],
        small_sums[4][None],
    )


def solution(mesh):
    return jax.shard_map(
        local,
        mesh=mesh,
        in_specs=(
            P(None, "ctx", None),
            P(None, "ctx"),
            P(None, "ctx", None),
            P("section", "ctx", "tensor"),
            P("section", "tensor"),
            P("section", None, None, "tensor"),
            P("section", None, "tensor"),
            P("section", "tensor", None),
            P("section", None),
            P("section", None, "tensor"),
            P("section", "tensor"),
            P("section", "tensor", None),
            P("section", None),
        ),
        out_specs=(
            P("section", None, "ctx", None),
            P("section", None, "ctx", None),
            P(None, "ctx"),
            P("section", "ctx", "tensor"),
            P("section", "tensor"),
            P("section", "ctx", None, "tensor"),
            P("section", None, "tensor"),
            P("section", "tensor", "ctx"),
            P("section", None),
            P("section", "ctx", "tensor"),
            P("section", "tensor"),
            P("section", "tensor", "ctx"),
            P("section", None),
        ),
        check_vma=False,
    )
```

```python
import functools
import math

import jax
import jax.numpy as jnp
from jax import lax
from jax.experimental import pallas as pl
from jax.experimental.pallas import tpu as pltpu
from jax.sharding import PartitionSpec as P

HD = 72
MB = 1
NMB = 3


EPSILON = 1e-06


MESH = pl.DeviceIdType.MESH
PIECES = 4
PIECE_ROWS = 16


def line_role(d, n, pieces, rows, x_ref, out_ref, acc, buf_l, buf_r, sems):
    send_r, send_l, recv_l, recv_r, back_send_r, back_send_l, back_recv = sems

    def part(j, s):
        return pl.ds((j * pieces + s) * rows, rows)

    def hop(src, dst, send_sem, recv_sem, to):
        return pltpu.make_async_remote_copy(
            src_ref=src,
            dst_ref=dst,
            send_sem=send_sem,
            recv_sem=recv_sem,
            device_id={"tensor": to},
            device_id_type=MESH,
        )

    def to_right(j, s, src):
        span = part(j, s)
        return hop(
            src.at[span], buf_l.at[span], send_r.at[j, s], recv_l.at[j, s], min(d + 1, n - 1)
        )

    def to_left(j, s, src):
        span = part(j, s)
        return hop(src.at[span], buf_r.at[span], send_l.at[j, s], recv_r.at[j, s], max(d - 1, 0))

    def back_right(j, s):
        span = part(j, s)
        return hop(
            out_ref.at[span],
            out_ref.at[span],
            back_send_r.at[j, s],
            back_recv.at[j, s],
            min(d + 1, n - 1),
        )

    def back_left(j, s):
        span = part(j, s)
        return hop(
            out_ref.at[span],
            out_ref.at[span],
            back_send_l.at[j, s],
            back_recv.at[j, s],
            max(d - 1, 0),
        )

    def done_at(j, s):
        return max(
            2 * j + (n - 1 - j) * pieces + s,
            2 * (n - 1 - j) + j * pieces + s,
        )

    steps = []
    for s in range(pieces):
        for j in range(d + 1, n):
            steps.append((2 * d + (n - 1 - j) * pieces + s, 0, j, s))
            steps.append((done_at(j, s) + 2 * (j - d), 3, j, s))
        for j in range(d):
            steps.append((2 * (n - 1 - d) + j * pieces + s, 1, j, s))
            steps.append((done_at(j, s) + 2 * (d - j), 3, j, s))
        steps.append((done_at(d, s), 2, d, s))
    steps.sort()
    sent = []
    for when, kind, j, s in steps:
        span = part(j, s)
        if kind == 0:
            src = x_ref
            if d > 0:
                to_right(j, s, x_ref).wait_recv()
                acc[span] = (
                    x_ref[span].astype(jnp.float32) + buf_l[span].astype(jnp.float32)
                ).astype(acc.dtype)
                src = acc
            sent.append(to_right(j, s, src))
            sent[-1].start()
        elif kind == 1:
            src = x_ref
            if d < n - 1:
                to_left(j, s, x_ref).wait_recv()
                acc[span] = (
                    x_ref[span].astype(jnp.float32) + buf_r[span].astype(jnp.float32)
                ).astype(acc.dtype)
                src = acc
            sent.append(to_left(j, s, src))
            sent[-1].start()
        elif kind == 2:
            total = x_ref[span].astype(jnp.float32)
            if d > 0:
                to_right(j, s, x_ref).wait_recv()
                total = total + buf_l[span].astype(jnp.float32)
            if d < n - 1:
                to_left(j, s, x_ref).wait_recv()
                total = total + buf_r[span].astype(jnp.float32)
            out_ref[span] = total.astype(out_ref.dtype)
            if d < n - 1:
                sent.append(back_right(j, s))
                sent[-1].start()
            if d > 0:
                sent.append(back_left(j, s))
                sent[-1].start()
        else:
            back_right(j, s).wait_recv()
            if j < d and d < n - 1:
                sent.append(back_right(j, s))
                sent[-1].start()
            if j > d and d > 0:
                sent.append(back_left(j, s))
                sent[-1].start()
    for copy in sent:
        copy.wait_send()


def line_sum_kernel(n, pieces, rows, x_ref, out_ref, acc, buf_l, buf_r, *sems):
    me = lax.axis_index("tensor")
    barrier = pltpu.get_barrier_semaphore()
    for d in range(n):

        @pl.when(me == d)
        def role():
            near = [at for at in (d - 1, d + 1) if 0 <= at < n]
            for at in near:
                pl.semaphore_signal(
                    barrier, inc=1, device_id={"tensor": at}, device_id_type=MESH
                )
            pl.semaphore_wait(barrier, len(near))
            line_role(d, n, pieces, rows, x_ref, out_ref, acc, buf_l, buf_r, sems)


def tensor_sum(term):
    n = lax.axis_size("tensor")
    if n == 1:
        return term
    total_rows, columns = term.shape
    pieces = max(1, min(PIECES, total_rows // (n * PIECE_ROWS)))
    rows = total_rows // (n * pieces)
    sem = pltpu.SemaphoreType.DMA((n, pieces))
    return pl.pallas_call(
        functools.partial(line_sum_kernel, n, pieces, rows),
        out_shape=jax.ShapeDtypeStruct(term.shape, term.dtype),
        in_specs=[pl.BlockSpec(memory_space=pltpu.VMEM)],
        out_specs=pl.BlockSpec(memory_space=pltpu.VMEM),
        scratch_shapes=[pltpu.VMEM(term.shape, term.dtype)] * 3 + [sem] * 7,
        compiler_params=pltpu.CompilerParams(collective_id=0, has_side_effects=True),
        name="tensor_sum",
    )(term)


def owner_sum_kernel(n, rows, x_ref, out_ref, held, send_sem, recv_sem):
    me = lax.axis_index("ctx")
    barrier = pltpu.get_barrier_semaphore()
    for step in range(1, n):
        pl.semaphore_signal(
            barrier, inc=1, device_id={"ctx": lax.rem(me + step, n)}, device_id_type=MESH
        )
    pl.semaphore_wait(barrier, n - 1)
    copies = []
    for step in range(1, n):
        peer = lax.rem(me + step, n)
        copy = pltpu.make_async_remote_copy(
            src_ref=x_ref.at[pl.ds(pl.multiple_of(peer * rows, rows), rows)],
            dst_ref=held.at[step - 1],
            send_sem=send_sem.at[step - 1],
            recv_sem=recv_sem.at[step - 1],
            device_id={"ctx": peer},
            device_id_type=MESH,
        )
        copy.start()
        copies.append(copy)
    own = pl.ds(pl.multiple_of(me * rows, rows), rows)
    out_ref[...] = x_ref[own].astype(jnp.float32)
    for step in range(1, n):
        copies[step - 1].wait_recv()
        out_ref[...] += held[step - 1].astype(jnp.float32)
    for copy in copies:
        copy.wait_send()


def owner_sum(parts):
    n = lax.axis_size("ctx")
    if n == 1:
        return parts.astype(jnp.float32)
    total_rows, columns = parts.shape
    rows = total_rows // n
    sem = pltpu.SemaphoreType.DMA((n - 1,))
    return pl.pallas_call(
        functools.partial(owner_sum_kernel, n, rows),
        out_shape=jax.ShapeDtypeStruct((rows, columns), jnp.float32),
        in_specs=[pl.BlockSpec(memory_space=pltpu.VMEM)],
        out_specs=pl.BlockSpec(memory_space=pltpu.VMEM),
        scratch_shapes=[pltpu.VMEM((n - 1, rows, columns), parts.dtype), sem, sem],
        compiler_params=pltpu.CompilerParams(collective_id=1, has_side_effects=True),
        name="owner_sum",
    )(parts)


def passed_along(shard, axis, by):
    devices = lax.axis_size(axis)
    pairs = [(i, i + by) for i in range(devices) if 0 <= i + by < devices]
    return lax.ppermute(shard, axis, pairs)


def layer_norm(values):
    centre = jnp.mean(values, axis=-1, keepdims=True)
    centred = values - centre
    variance = jnp.mean(centred * centred, axis=-1, keepdims=True)
    inverse = lax.rsqrt(variance + EPSILON)
    return (centred * inverse, inverse)


def norm_back(normed, inverse, upstream):
    mean_grad = jnp.mean(upstream, axis=-1, keepdims=True)
    mean_cross = jnp.mean(upstream * normed, axis=-1, keepdims=True)
    return inverse * (upstream - mean_grad - normed * mean_cross)


def gelu_back(pre_act, upstream):
    unused_out, pullback = jax.vjp(
        lambda pre_value: jax.nn.gelu(pre_value, approximate=True), pre_act
    )
    return pullback(upstream)[0]


def head_view(array):
    return array.reshape(array.shape[0], array.shape[1], array.shape[2] // HD, HD)


def attend(queries, keys_all, values_all):
    softmax_scale = 1.0 / math.sqrt(HD)
    scores = (
        jnp.einsum(
            "bqhd,bkhd->bhqk",
            head_view(queries),
            head_view(keys_all),
            preferred_element_type=jnp.float32,
        )
        * softmax_scale
    )
    row_peak = jnp.max(scores, axis=-1, keepdims=True)
    log_total = row_peak + jnp.log(jnp.sum(jnp.exp(scores - row_peak), axis=-1, keepdims=True))
    prob_bf = jnp.exp(scores - log_total).astype(jnp.bfloat16)
    context = jnp.einsum(
        "bhqk,bkhd->bqhd", prob_bf, head_view(values_all), preferred_element_type=jnp.float32
    )
    return (context.astype(jnp.bfloat16).reshape(queries.shape), log_total)


def row_delta(context, context_grad):
    delta_rows = jnp.sum(
        head_view(context_grad).astype(jnp.float32) * head_view(context).astype(jnp.float32),
        axis=-1,
    )
    return jnp.transpose(delta_rows, (0, 2, 1))[..., None]


def score_terms(query_heads, key_heads, value_heads, grad_heads, log_total, delta_rows):
    softmax_scale = 1.0 / math.sqrt(HD)
    scores = (
        jnp.einsum("bqhd,bkhd->bhqk", query_heads, key_heads, preferred_element_type=jnp.float32)
        * softmax_scale
    )
    prob_full = jnp.exp(scores - log_total)
    prob_grad = jnp.einsum(
        "bqhd,bkhd->bhqk", grad_heads, value_heads, preferred_element_type=jnp.float32
    )
    score_grad = (prob_full * (prob_grad - delta_rows)).astype(jnp.bfloat16)
    return (prob_full, score_grad)


def key_side(query_heads, grad_heads, prob_full, score_grad, key_shape):
    softmax_scale = 1.0 / math.sqrt(HD)
    prob_bf = prob_full.astype(jnp.bfloat16)
    key_part = (
        jnp.einsum("bhqk,bqhd->bkhd", score_grad, query_heads, preferred_element_type=jnp.float32)
        * softmax_scale
    )
    value_part = jnp.einsum(
        "bhqk,bqhd->bkhd", prob_bf, grad_heads, preferred_element_type=jnp.float32
    )
    return (key_part.reshape(key_shape), value_part.reshape(key_shape))


def attention_grads(queries, keys_all, values_all, log_total, context, context_grad):
    softmax_scale = 1.0 / math.sqrt(HD)
    query_heads = head_view(queries)
    key_heads = head_view(keys_all)
    grad_heads = head_view(context_grad)
    delta_rows = row_delta(context, context_grad)
    prob_full, score_grad = score_terms(
        query_heads, key_heads, head_view(values_all), grad_heads, log_total, delta_rows
    )
    query_grad = (
        jnp.einsum("bhqk,bkhd->bqhd", score_grad, key_heads, preferred_element_type=jnp.float32)
        * softmax_scale
    ).reshape(queries.shape)
    key_part, value_part = key_side(query_heads, grad_heads, prob_full, score_grad, keys_all.shape)
    cols = queries.shape[-1]
    both = jnp.concatenate([key_part, value_part], axis=-1).astype(jnp.bfloat16)
    owned = owner_sum(both.reshape(-1, 2 * cols)).reshape(*queries.shape[:2], 2 * cols)
    key_grad, value_grad = owned[..., :cols], owned[..., cols:]
    return (query_grad, key_grad, value_grad)


def forward_block(block_in, mod_rows, weights):
    w_qkv, b_qv, w_out, b_out, w_fc1, b_fc1, w_fc2, b_fc2 = weights
    latent_count, token_count, model_width = block_in.shape
    row_count = latent_count * token_count
    local_cols = w_qkv.shape[-1]
    residual = block_in.astype(jnp.float32)
    normed_a, inverse_a = layer_norm(residual)
    attn_in = (normed_a * (1.0 + mod_rows[:, 1, None, :]) + mod_rows[:, 0, None, :]).astype(
        jnp.bfloat16
    )
    projected = jnp.dot(
        attn_in.reshape(row_count, model_width),
        w_qkv.reshape(model_width, 3 * local_cols),
        preferred_element_type=jnp.float32,
    ).reshape(latent_count, token_count, 3, local_cols)
    queries = (projected[:, :, 0] + b_qv[0]).astype(jnp.bfloat16)
    key_rows = projected[:, :, 1].astype(jnp.bfloat16)
    values = (projected[:, :, 2] + b_qv[1]).astype(jnp.bfloat16)
    both = lax.all_gather(
        jnp.concatenate([key_rows, values], axis=-1), "ctx", axis=1, tiled=True
    )
    keys_all, values_all = both[..., :local_cols], both[..., local_cols:]
    context, log_total = attend(queries, keys_all, values_all)
    attn_term = jnp.dot(
        context.reshape(row_count, local_cols), w_out, preferred_element_type=jnp.float32
    )
    attn_out = (
        tensor_sum(attn_term.astype(jnp.bfloat16))
        .astype(jnp.float32)
        .reshape(block_in.shape)
        + b_out
    )
    middle = residual + mod_rows[:, 2, None, :] * attn_out
    normed_m, inverse_m = layer_norm(middle)
    mlp_in = (normed_m * (1.0 + mod_rows[:, 4, None, :]) + mod_rows[:, 3, None, :]).astype(
        jnp.bfloat16
    )
    pre_act = (
        jnp.dot(mlp_in.reshape(row_count, model_width), w_fc1, preferred_element_type=jnp.float32)
        + b_fc1
    )
    hidden = jax.nn.gelu(pre_act, approximate=True).astype(jnp.bfloat16)
    mlp_term = jnp.dot(hidden, w_fc2, preferred_element_type=jnp.float32)
    mlp_out = (
        tensor_sum(mlp_term.astype(jnp.bfloat16))
        .astype(jnp.float32)
        .reshape(block_in.shape)
        + b_fc2
    )
    block_res = (middle + mod_rows[:, 5, None, :] * mlp_out).astype(jnp.bfloat16)
    stored = (
        normed_a,
        inverse_a,
        attn_in,
        queries,
        keys_all,
        values_all,
        log_total,
        context,
        attn_out,
        normed_m,
        inverse_m,
        mlp_in,
        pre_act,
        hidden,
        mlp_out,
    )
    return (block_res, stored)


def backward_block(upstream, stored, mod_rows, weights):
    w_qkv, b_qv, w_out, b_out, w_fc1, b_fc1, w_fc2, b_fc2 = weights
    (
        normed_a,
        inverse_a,
        attn_in,
        queries,
        keys_all,
        values_all,
        log_total,
        context,
        attn_out,
        normed_m,
        inverse_m,
        mlp_in,
        pre_act,
        hidden,
        mlp_out,
    ) = stored
    latent_count, token_count, model_width = upstream.shape
    row_count = latent_count * token_count
    local_cols = queries.shape[-1]
    gate_m_grad = jnp.sum(upstream * mlp_out, axis=1)
    mlp_grad = upstream * mod_rows[:, 5, None, :]
    mlp_grad_b = mlp_grad.reshape(row_count, model_width).astype(jnp.bfloat16)
    grad_b2 = jnp.sum(mlp_grad, axis=(0, 1))
    pre_grad = gelu_back(pre_act, jnp.dot(mlp_grad_b, w_fc2.T, preferred_element_type=jnp.float32))
    pre_grad_b = pre_grad.astype(jnp.bfloat16)
    grad_b1 = jnp.sum(pre_grad, axis=0)
    mlp_in_grad = (
        tensor_sum(
            jnp.dot(pre_grad_b, w_fc1.T, preferred_element_type=jnp.float32).astype(jnp.bfloat16)
        )
        .astype(jnp.float32)
        .reshape(upstream.shape)
    )
    shift_m_grad = jnp.sum(mlp_in_grad, axis=1)
    scale_m_grad = jnp.sum(mlp_in_grad * normed_m, axis=1)
    middle_grad = upstream + norm_back(
        normed_m, inverse_m, mlp_in_grad * (1.0 + mod_rows[:, 4, None, :])
    )
    gate_a_grad = jnp.sum(middle_grad * attn_out, axis=1)
    attn_grad = middle_grad * mod_rows[:, 2, None, :]
    attn_grad_b = attn_grad.reshape(row_count, model_width).astype(jnp.bfloat16)
    grad_bo = jnp.sum(attn_grad, axis=(0, 1))
    context_grad = (
        jnp.dot(attn_grad_b, w_out.T, preferred_element_type=jnp.float32)
        .astype(jnp.bfloat16)
        .reshape(queries.shape)
    )
    query_grad, key_grad, value_grad = attention_grads(
        queries, keys_all, values_all, log_total, context, context_grad
    )
    grad_bqv = jnp.stack([jnp.sum(query_grad, axis=(0, 1)), jnp.sum(value_grad, axis=(0, 1))])
    qkv_grad_b = (
        jnp.stack([query_grad, key_grad, value_grad], axis=2)
        .astype(jnp.bfloat16)
        .reshape(row_count, 3 * local_cols)
    )
    attn_in_grad = (
        tensor_sum(
            jnp.dot(
                qkv_grad_b,
                w_qkv.reshape(model_width, 3 * local_cols).T,
                preferred_element_type=jnp.float32,
            ).astype(jnp.bfloat16)
        )
        .astype(jnp.float32)
        .reshape(upstream.shape)
    )
    shift_a_grad = jnp.sum(attn_in_grad, axis=1)
    scale_a_grad = jnp.sum(attn_in_grad * normed_a, axis=1)
    input_grad = middle_grad + norm_back(
        normed_a, inverse_a, attn_in_grad * (1.0 + mod_rows[:, 1, None, :])
    )
    mod_grad = jnp.stack(
        [shift_a_grad, scale_a_grad, gate_a_grad, shift_m_grad, scale_m_grad, gate_m_grad], axis=1
    )
    return (
        input_grad,
        mod_grad,
        (grad_bqv, grad_bo, grad_b1, grad_b2),
        (
            (attn_in.reshape(row_count, model_width), qkv_grad_b),
            (context.reshape(row_count, local_cols), attn_grad_b),
            (mlp_in.reshape(row_count, model_width), pre_grad_b),
            (hidden, mlp_grad_b),
        ),
    )


def local(
    latents,
    condition,
    cotangent,
    w_ada,
    b_ada,
    w_qkv,
    b_qv,
    w_out,
    b_out,
    w_fc1,
    b_fc1,
    w_fc2,
    b_fc2,
):
    weights = (w_qkv[0], b_qv[0], w_out[0], b_out[0], w_fc1[0], b_fc1[0], w_fc2[0], b_fc2[0])
    section_index = lax.axis_index("section")
    latent_total, token_count, model_width = latents.shape
    width_cols = b_ada.shape[-1]
    col_offset = lax.axis_index("tensor") * width_cols
    cond_act = jax.nn.silu(condition).astype(jnp.bfloat16)
    mod_part = jnp.dot(cond_act, w_ada[0], preferred_element_type=jnp.float32)
    mod_local = lax.psum(mod_part, "ctx") + b_ada[0]
    modulation = lax.all_gather(mod_local, "tensor", axis=1, tiled=True).reshape(
        latent_total, 6, model_width
    )
    received = jnp.zeros((MB, token_count, model_width), jnp.bfloat16)
    block_out = jnp.zeros_like(latents)
    kept_states = []
    for forward_tick in range(NMB + 1):
        micro_index = forward_tick - section_index
        is_valid = (micro_index >= 0) & (micro_index < NMB)
        offset = jnp.clip(micro_index, 0, NMB - 1) * MB
        own_rows = lax.dynamic_slice_in_dim(latents, offset, MB, 0)
        block_in = jnp.where(section_index == 0, own_rows, received)
        mod_rows = lax.dynamic_slice_in_dim(modulation, offset, MB, 0)
        block_res, stored = forward_block(block_in, mod_rows, weights)
        kept_states.append(stored)
        previous = lax.dynamic_slice_in_dim(block_out, offset, MB, 0)
        block_out = lax.dynamic_update_slice_in_dim(
            block_out, jnp.where(is_valid, block_res, previous), offset, 0
        )
        if forward_tick < NMB:
            received = passed_along(block_res, "section", 1)
    in_grads = jnp.zeros(latents.shape, jnp.float32)
    mod_grads = jnp.zeros((latent_total, width_cols), jnp.float32)
    pairs = []
    small_local = tuple(
        (
            jnp.zeros(weight.shape, jnp.float32)
            for weight in (weights[1], weights[3], weights[5], weights[7])
        )
    )
    grad_received = jnp.zeros((MB, token_count, model_width), jnp.float32)
    for back_tick in range(NMB + 1):
        forward_tick = NMB - back_tick
        micro_index = forward_tick - section_index
        is_valid = (micro_index >= 0) & (micro_index < NMB)
        offset = jnp.clip(micro_index, 0, NMB - 1) * MB
        own_cot = lax.dynamic_slice_in_dim(cotangent, offset, MB, 0).astype(jnp.float32)
        upstream = jnp.where(section_index == 1, own_cot, grad_received)
        mod_rows = lax.dynamic_slice_in_dim(modulation, offset, MB, 0)
        stored = kept_states[forward_tick]
        input_grad, mod_grad, grad_terms, grad_pairs = backward_block(
            upstream, stored, mod_rows, weights
        )
        pairs.append(
            tuple(
                (left, jnp.where(is_valid, right, jnp.zeros_like(right)))
                for left, right in grad_pairs
            )
        )
        masked = tuple((jnp.where(is_valid, term, 0.0) for term in grad_terms))
        previous = lax.dynamic_slice_in_dim(in_grads, offset, MB, 0)
        in_grads = lax.dynamic_update_slice_in_dim(
            in_grads, jnp.where(is_valid, input_grad, previous), offset, 0
        )
        mod_piece = lax.dynamic_slice_in_dim(
            mod_grad.reshape(MB, 6 * model_width), col_offset, width_cols, 1
        )
        prior = lax.dynamic_slice_in_dim(mod_grads, offset, MB, 0)
        mod_grads = lax.dynamic_update_slice_in_dim(
            mod_grads, jnp.where(is_valid, mod_piece, prior), offset, 0
        )
        small_local = tuple(total + term for total, term in zip(small_local, masked))
        if back_tick < NMB:
            grad_received = passed_along(input_grad.astype(jnp.bfloat16), "section", -1).astype(
                input_grad.dtype
            )
    big_local = tuple(
        jnp.dot(
            jnp.concatenate([tick[which][0] for tick in pairs], axis=0).T,
            jnp.concatenate([tick[which][1] for tick in pairs], axis=0),
            preferred_element_type=jnp.float32,
        )
        for which in range(4)
    )
    big_local = (big_local[0].reshape(weights[0].shape),) + big_local[1:]
    shares = (
        lax.psum_scatter(
            big_local[0].astype(jnp.bfloat16), "ctx", scatter_dimension=0, tiled=True
        ).astype(jnp.float32),
        lax.psum_scatter(
            big_local[1].astype(jnp.bfloat16), "ctx", scatter_dimension=1, tiled=True
        ).astype(jnp.float32),
        lax.psum_scatter(
            big_local[2].astype(jnp.bfloat16), "ctx", scatter_dimension=0, tiled=True
        ).astype(jnp.float32),
        lax.psum_scatter(
            big_local[3].astype(jnp.bfloat16), "ctx", scatter_dimension=1, tiled=True
        ).astype(jnp.float32),
    )
    small_sums = lax.psum(
        (mod_grads, small_local[0], small_local[1], small_local[2], small_local[3]), "ctx"
    )
    mod_total = small_sums[0]
    mod_rounded = mod_total.astype(jnp.bfloat16)
    grad_w_ada = jnp.dot(cond_act.T, mod_rounded, preferred_element_type=jnp.float32)[None]
    grad_b_ada = jnp.sum(mod_total, axis=0)[None]
    cond_part = jnp.dot(mod_rounded, w_ada[0].T, preferred_element_type=jnp.float32)
    cond_sum = lax.psum(cond_part, ("section", "tensor"))
    sigmoid_c = jax.nn.sigmoid(condition)
    cond_grad = cond_sum * sigmoid_c * (1.0 + condition * (1.0 - sigmoid_c))
    return (
        block_out[None],
        in_grads[None],
        cond_grad,
        grad_w_ada,
        grad_b_ada,
        shares[0][None],
        small_sums[1][None],
        shares[1][None],
        small_sums[2][None],
        shares[2][None],
        small_sums[3][None],
        shares[3][None],
        small_sums[4][None],
    )


def solution(mesh):
    return jax.shard_map(
        local,
        mesh=mesh,
        in_specs=(
            P(None, "ctx", None),
            P(None, "ctx"),
            P(None, "ctx", None),
            P("section", "ctx", "tensor"),
            P("section", "tensor"),
            P("section", None, None, "tensor"),
            P("section", None, "tensor"),
            P("section", "tensor", None),
            P("section", None),
            P("section", None, "tensor"),
            P("section", "tensor"),
            P("section", "tensor", None),
            P("section", None),
        ),
        out_specs=(
            P("section", None, "ctx", None),
            P("section", None, "ctx", None),
            P(None, "ctx"),
            P("section", "ctx", "tensor"),
            P("section", "tensor"),
            P("section", "ctx", None, "tensor"),
            P("section", None, "tensor"),
            P("section", "tensor", "ctx"),
            P("section", None),
            P("section", "ctx", "tensor"),
            P("section", "tensor"),
            P("section", "tensor", "ctx"),
            P("section", None),
        ),
        check_vma=False,
    )
```
